32 devices in a mesh: docs: 8 (over z, x), topics: 4 (over y, core).
Axes of the slice: x: 2, y: 2, z: 4, core: 2. Of those that a mesh axis runs over, the one named last changes fastest.
Arguments:
- log_beta: bfloat16 [262144, 2048], P('docs', 'topics'), may hold values from -250 to -4
- gamma_init: float32 [128, 2048], P('docs', 'topics'), may hold values from 0.05 to 5
- topic_prior: float32 [2048], P('topics'), may hold values from 0.02 to 0.5
- word_block: int32 [128, 256, 1], P('docs'), may hold values from 0 to 7; in each aligned block of 4096 rows (0 to 4095, 4096 to 8191, ..., all dimensions but the last counted through in order) at most 1024 rows name the same one
- word_row: int32 [128, 256], P('docs'), may hold values from 0 to 32767
- counts: int32 [128, 256], P('docs'), may hold values from 0 to 2
Outputs:
- doc_gamma: float32 [128, 2048], P('docs', 'topics')
- sstats: float32 [262144, 2048], P('docs', 'topics')
The draws below stay inside these ranges and needn't reach their ends.
Inputs may be any that keep to these rules, and one draw needn't show every extreme that they name: `word_block`: among the token slots of one device's 16 documents, at most 1024 name the same vocabulary block, and some block is named by exactly 1024 of them on some device. `counts`: A count of 0 marks an empty slot.
All inputs are finite; a program needn't handle non-finite values.
Results may differ from the reference program's by a relative error of at most 0.0003.
Values may be sent and summed in bfloat16 or wider, within the bound.
No kernel may reach another device: no remote copies, remote signals or barrier semaphores. Data moves between devices by JAX's collectives and lax.ppermute only.
A program may use at most 192 MiB of HBM per device.

```python
import math
import jax
import jax.numpy as jnp
import numpy as np
from jax import lax

K = 2048
VOCAB = 262144
LEN = 256
ITERS = 3
DOC_DEV = 16
DOCS = 128
VOC_DEV = 32768
CAP = 1024
N_DOCS = 8


def draw_log_beta(key, part):
    values = jax.random.uniform(key, (VOCAB, K), jnp.float32, -14.0, -4.0)
    return values.astype(jnp.bfloat16)


def place_ends(result, key, least, largest):
    spot = [jax.random.randint(jax.random.fold_in(key, axis), (), 0, length) for axis, length in enumerate(result.shape)]
    widest = result.shape.index(max(result.shape))
    beside = spot[:widest] + [(spot[widest] + 1) % result.shape[widest]] + spot[widest + 1:]
    return result.at[tuple(spot)].set(least).at[tuple(beside)].set(largest)


def levels(key, extent, cuts, low, top_value):
    level, own = 1.0, jax.random.fold_in(key, 6)
    for dim, parts in cuts:
        heights = jnp.exp(jax.random.uniform(jax.random.fold_in(own, dim), (parts,), jnp.float32, low / len(cuts), top_value / len(cuts)))
        level = level * jnp.repeat(heights, extent[dim] // parts).reshape([-1 if axis == dim else 1 for axis in range(len(extent))])
    return level


def assign_block(rng, own, number, rows, count, top, bound, slope):
    order = jax.random.permutation(rng, count)
    packed, common = load_shares(count, rows * top, bound, slope, True), load_shares(count, rows * top, bound, slope, False)
    places = jnp.arange(count)

    def named(lengths, offset_by):
        used = int((lengths > 0).sum())
        fixed = max(1, used // 4)
        shifted = fixed + (places - fixed + offset_by * (used - fixed)) % max(1, count - fixed)
        return jnp.zeros((count,), jnp.int32).at[order[jnp.where(places < fixed, places, shifted)]].set(jnp.asarray(lengths, jnp.int32))

    lengths = jnp.where(number % 4 == 0, named(packed, number // 4), named(common, number - number // 4 - 1))
    mixed = jax.random.permutation(jax.random.fold_in(own, 3), count)
    source_of, receiver = mixed[0:count // 2 * 2:2], mixed[1:count // 2 * 2:2]
    room = jnp.minimum(lengths[source_of] - 1, bound - lengths[receiver]) // 2
    room = jnp.where((source_of == order[0]) | (receiver == order[0]) | (lengths[receiver] == 0), 0, jnp.maximum(room, 0))
    shifted = jax.random.randint(jax.random.fold_in(own, 4), (count // 2,), 0, 1 << 20) % (room + 1)
    lengths = lengths.at[source_of].add(-shifted).at[receiver].add(shifted)
    labels = jnp.searchsorted(jnp.cumsum(lengths), jnp.arange(rows * top), side="right").astype(jnp.int32)
    listing = labels.reshape(top, rows).T
    listing = listing[jax.random.permutation(jax.random.fold_in(own, 1), rows)]
    offset_by = jax.random.randint(jax.random.fold_in(own, 2), (rows, 1), 0, top)
    return jnp.take_along_axis(listing, (jnp.arange(top)[None, :] + offset_by) % top, axis=1)


def load_shares(number_of, total, bound, skew, full):
    weights = [(1 << 20) // math.isqrt(standing ** skew) + 1 for standing in range(1, number_of + 1)]
    largest = bound if full else min(bound, max(-(-total // number_of), total * weights[0] // sum(weights)))
    least = 1 if total - largest >= number_of - 1 else 0
    given, rest = [largest] + [least] * (number_of - 1), total - largest - least * (number_of - 1)
    while rest > 0:
        free = [i for i in range(1, number_of) if given[i] < largest] or [i for i in range(1, number_of) if given[i] < bound]
        pool, budget = sum([weights[i] for i in free]), rest
        for i in free:
            addition = min(bound - given[i], max(1, budget * weights[i] // pool), rest)
            given[i] = given[i] + addition
            rest = rest - addition
    return np.array(given)


def setup_inputs(seed: int = 0) -> dict:
    splits = jax.random.split(jax.random.key(seed), 7)
    log_beta = draw_log_beta(jax.random.fold_in(splits[6], 71), 0)
    gamma_init = jnp.clip(jnp.exp(math.log(5.0) - 4.6051702 * jax.random.uniform(splits[1], (DOCS, K), jnp.float32) ** levels(splits[1], (DOCS, K), ((0, 8), (1, 4)), -0.2, 0.2)), 0.05, 5.0)
    topic_prior = jnp.clip(jnp.exp(math.log(0.5) - 3.218876 * jax.random.uniform(splits[2], (K,), jnp.float32) ** levels(splits[2], (K,), ((0, 4),), -0.2, 0.2)), 0.02, 0.5)
    word_block_keys = jax.random.split(jax.random.fold_in(splits[3], 1), DOCS * LEN // (DOC_DEV * LEN))
    word_block_turns = jax.random.permutation(jax.random.fold_in(splits[3], 3), DOCS * LEN // (DOC_DEV * LEN))
    word_block = jax.vmap(lambda own, number: assign_block(jax.random.fold_in(splits[3], 2), own, number, DOC_DEV * LEN, N_DOCS, 1, CAP, 1))(word_block_keys, word_block_turns).reshape((DOCS, LEN, 1))
    word_row = place_ends(jax.random.randint(splits[4], (DOCS, LEN), 0, VOC_DEV), jax.random.fold_in(splits[4], 1), 0, VOC_DEV - 1).astype(jnp.int32)
    counts = place_ends(jax.random.randint(splits[5], (DOCS, LEN), 0, 3), jax.random.fold_in(splits[5], 1), 0, 2).astype(jnp.int32)
    return {"log_beta": log_beta, "gamma_init": gamma_init, "topic_prior": topic_prior, "word_block": word_block, "word_row": word_row, "counts": counts}


def expect_log(doc_gamma):
    return lax.digamma(doc_gamma)


def token_weights(log_theta, beta_rows):
    scores = log_theta[:, None, :] + beta_rows.astype(jnp.float32)
    row_max = jnp.max(scores, axis=2)
    exp_mass = jnp.sum(jnp.exp(scores - row_max[:, :, None]), axis=2)
    log_norm = row_max + jnp.log(exp_mass)
    return jnp.exp(scores - log_norm[:, :, None])


def reference(log_beta, gamma_init, topic_prior, word_block, word_row, counts):
    word_ids = word_block[:, :, 0] * VOC_DEV + word_row
    word_sets = word_ids.reshape(N_DOCS, DOC_DEV, LEN)
    count_sets = counts.astype(jnp.float32).reshape(N_DOCS, DOC_DEV, LEN)
    doc_gamma = gamma_init
    for sweep_index in range(ITERS):
        log_theta = expect_log(doc_gamma).reshape(N_DOCS, DOC_DEV, K)

        def renew_block(pieces):
            theta_part, word_part, count_part = pieces
            topic_share = token_weights(theta_part, log_beta[word_part])
            return topic_prior[None, :] + jnp.einsum("dn,dnk->dk", count_part, topic_share, precision=lax.Precision.HIGHEST)

        doc_gamma = lax.map(renew_block, (log_theta, word_sets, count_sets)).reshape(DOCS, K)
    final_theta = expect_log(doc_gamma).reshape(N_DOCS, DOC_DEV, K)

    def accumulate(doc_block, sstats):
        word_part = word_sets[doc_block]
        topic_share = token_weights(final_theta[doc_block], log_beta[word_part])
        contrib = count_sets[doc_block][:, :, None] * topic_share
        return sstats.at[word_part.reshape(-1)].add(contrib.reshape(-1, K))

    sstats = lax.fori_loop(0, N_DOCS, accumulate, jnp.zeros((VOCAB, K), jnp.float32))
    return doc_gamma, sstats
```

```python
import jax
import jax.numpy as jnp
from jax import lax
from jax.experimental import pallas as pl
from jax.experimental.pallas import tpu as pltpu
from jax.sharding import PartitionSpec as P

ITERS = 3
COUNT_SPAN = 4
NT = (((1,), (1,)), ((), ()))
TN = (((0,), (0,)), ((), ()))
NN = (((1,), (0,)), ((), ()))


def spread(part, axis):
    size = lax.axis_size(axis)
    return lax.all_to_all(
        jnp.broadcast_to(part[None], (size,) + part.shape), axis, split_axis=0, concat_axis=0, tiled=True
    )


def split_two(values):
    high = values.astype(jnp.bfloat16)
    return high, (values - high.astype(jnp.float32)).astype(jnp.bfloat16)


def dot(left, right, dims):
    return lax.dot_general(left, right, dims, preferred_element_type=jnp.float32)


def params(megabytes=56):
    return pltpu.CompilerParams(
        dimension_semantics=("arbitrary",), vmem_limit_bytes=megabytes * 1024 * 1024
    )


def row_hits(rows, base, extent):
    places = lax.broadcasted_iota(jnp.int32, (extent, rows.shape[1]), 0)
    return jnp.where(places == rows - base, 1.0, 0.0).astype(jnp.bfloat16)


def gather_rows(log_beta, rows, starts, block, chunk):
    vocab, cols = log_beta.shape
    chunks = rows.shape[0]

    def body(starts_ref, rows_ref, beta_ref, out_ref):
        step = pl.program_id(0)

        @pl.when(step == 0)
        def _():
            out_ref[...] = jnp.zeros_like(out_ref)

        low, high = starts_ref[step], starts_ref[step + 1]

        @pl.when(high > low)
        def _():
            def visit(at, carry):
                hits = row_hits(rows_ref[pl.ds(at, 1), :], step * block, block)
                found = dot(hits, beta_ref[...], TN).astype(jnp.bfloat16)
                window = pl.ds(pl.multiple_of(at * chunk, chunk), chunk)
                out_ref[window, :] = out_ref[window, :] + found
                return carry

            lax.fori_loop(low // chunk, (high + chunk - 1) // chunk, visit, 0)

    return pl.pallas_call(
        body,
        grid_spec=pltpu.PrefetchScalarGridSpec(
            num_scalar_prefetch=1,
            grid=(vocab // block,),
            in_specs=[
                pl.BlockSpec((chunks, chunk), lambda i, s: (0, 0)),
                pl.BlockSpec((block, cols), lambda i, s: (i, 0)),
            ],
            out_specs=pl.BlockSpec((chunks * chunk, cols), lambda i, s: (0, 0)),
        ),
        out_shape=jax.ShapeDtypeStruct((chunks * chunk, cols), jnp.bfloat16),
        compiler_params=params(),
        name="gather_rows",
    )(starts, rows, log_beta)


def last_used(used, tile):
    return jnp.maximum((used + tile - 1) // tile - 1, 0)


def shifted_exp(found, used, tile):
    slots, cols = found.shape

    def body(used_ref, found_ref, high_ref, low_ref, top_ref):
        @pl.when(pl.program_id(0) <= last_used(used_ref[0], tile))
        def _():
            values = found_ref[...].astype(jnp.float32)
            top = jnp.max(values, axis=1, keepdims=True)
            high_ref[...], low_ref[...] = split_two(jnp.exp(values - top))
            top_ref[0] = jnp.transpose(jnp.broadcast_to(top, (tile, 128)))[0:1, :]

    def at(i, used):
        return (jnp.minimum(i, last_used(used[0], tile)), 0)

    return pl.pallas_call(
        body,
        grid_spec=pltpu.PrefetchScalarGridSpec(
            num_scalar_prefetch=1,
            grid=(slots // tile,),
            in_specs=[pl.BlockSpec((tile, cols), at)],
            out_specs=[
                pl.BlockSpec((tile, cols), at),
                pl.BlockSpec((tile, cols), at),
                pl.BlockSpec((1, 1, tile), lambda i, used: at(i, used) + (0,)),
            ],
        ),
        out_shape=[
            jax.ShapeDtypeStruct((slots, cols), jnp.bfloat16),
            jax.ShapeDtypeStruct((slots, cols), jnp.bfloat16),
            jax.ShapeDtypeStruct((slots // tile, 1, tile), jnp.float32),
        ],
        compiler_params=params(),
        name="shifted_exp",
    )(used, found)


def slot_mass(theta, beta_high, beta_low, docs, used, tile):
    slots, cols = beta_high.shape
    doc_rows = theta.shape[0]

    def body(used_ref, theta_ref, high_ref, low_ref, docs_ref, mass_ref):
        @pl.when(pl.program_id(0) <= last_used(used_ref[0], tile))
        def _():
            theta_high, theta_low = split_two(theta_ref[...])
            mass = dot(theta_high, high_ref[...], NT)
            mass = mass + dot(theta_low, high_ref[...], NT)
            mass = mass + dot(theta_high, low_ref[...], NT)
            places = lax.broadcasted_iota(jnp.int32, (doc_rows, tile), 0)
            mass_ref[0] = jnp.sum(jnp.where(places == docs_ref[0], mass, 0.0), axis=0, keepdims=True)

    def at(i, used):
        return (jnp.minimum(i, last_used(used[0], tile)), 0)

    def line(i, used):
        return at(i, used) + (0,)

    return pl.pallas_call(
        body,
        grid_spec=pltpu.PrefetchScalarGridSpec(
            num_scalar_prefetch=1,
            grid=(slots // tile,),
            in_specs=[
                pl.BlockSpec((doc_rows, cols), lambda i, used: (0, 0)),
                pl.BlockSpec((tile, cols), at),
                pl.BlockSpec((tile, cols), at),
                pl.BlockSpec((1, 1, tile), line),
            ],
            out_specs=pl.BlockSpec((1, 1, tile), line),
        ),
        out_shape=jax.ShapeDtypeStruct((slots // tile, 1, tile), jnp.float32),
        compiler_params=params(),
        name="slot_mass",
    )(used, theta, beta_high, beta_low, docs)


def doc_sums(weights, docs, beta_high, beta_low, doc_rows, used, tile):
    slots, cols = beta_high.shape

    def body(used_ref, weights_ref, docs_ref, high_ref, low_ref, sums_ref):
        step = pl.program_id(0)

        @pl.when(step == 0)
        def _():
            sums_ref[...] = jnp.zeros_like(sums_ref)

        @pl.when(step <= last_used(used_ref[0], tile))
        def _():
            places = lax.broadcasted_iota(jnp.int32, (doc_rows, tile), 0)
            share_high, share_low = split_two(jnp.where(places == docs_ref[0], weights_ref[0], 0.0))
            sums = dot(share_high, high_ref[...], NN)
            sums = sums + dot(share_low, high_ref[...], NN)
            sums_ref[...] += sums + dot(share_high, low_ref[...], NN)

    def at(i, used):
        return (jnp.minimum(i, last_used(used[0], tile)), 0)

    def line(i, used):
        return at(i, used) + (0,)

    return pl.pallas_call(
        body,
        grid_spec=pltpu.PrefetchScalarGridSpec(
            num_scalar_prefetch=1,
            grid=(slots // tile,),
            in_specs=[
                pl.BlockSpec((1, 1, tile), line),
                pl.BlockSpec((1, 1, tile), line),
                pl.BlockSpec((tile, cols), at),
                pl.BlockSpec((tile, cols), at),
            ],
            out_specs=pl.BlockSpec((doc_rows, cols), lambda i, used: (0, 0)),
        ),
        out_shape=jax.ShapeDtypeStruct((doc_rows, cols), jnp.float32),
        compiler_params=params(),
        name="doc_sums",
    )(used, weights, docs, beta_high, beta_low)


def word_sums(theta, weights, docs, rows, beta_high, beta_low, starts, vocab, block, chunk):
    slots, cols = beta_high.shape
    doc_rows = theta.shape[0]
    chunks = slots // chunk

    def body(starts_ref, theta_ref, weights_ref, docs_ref, rows_ref, high_ref, low_ref, out_ref):
        step = pl.program_id(0)
        out_ref[...] = jnp.zeros_like(out_ref)
        low, high = starts_ref[step], starts_ref[step + 1]

        @pl.when(high > low)
        def _():
            theta_high, theta_low = split_two(theta_ref[...])

            def visit(at, carry):
                window = pl.ds(pl.multiple_of(at * chunk, chunk), chunk)
                line = pl.ds(at, 1)
                places = lax.broadcasted_iota(jnp.int32, (doc_rows, chunk), 0)
                scale_high, scale_low = split_two(
                    jnp.where(places == docs_ref[line, :], weights_ref[line, :], 0.0)
                )
                scaled = dot(scale_high, theta_high, TN)
                scaled = scaled + dot(scale_low, theta_high, TN)
                scaled = scaled + dot(scale_high, theta_low, TN)
                beta = high_ref[window, :].astype(jnp.float32) + low_ref[window, :].astype(jnp.float32)
                term_high, term_low = split_two(scaled * beta)
                hits = row_hits(rows_ref[line, :], step * block, block)
                out_ref[...] += dot(hits, term_high, NN) + dot(hits, term_low, NN)
                return carry

            lax.fori_loop(low // chunk, (high + chunk - 1) // chunk, visit, 0)

    def whole(shape):
        return pl.BlockSpec(shape, lambda i, s: (0, 0), pipeline_mode=pl.Buffered(1))

    return pl.pallas_call(
        body,
        grid_spec=pltpu.PrefetchScalarGridSpec(
            num_scalar_prefetch=1,
            grid=(vocab // block,),
            in_specs=[
                whole((doc_rows, cols)),
                whole((chunks, chunk)),
                whole((chunks, chunk)),
                whole((chunks, chunk)),
                whole((slots, cols)),
                whole((slots, cols)),
            ],
            out_specs=pl.BlockSpec((block, cols), lambda i, s: (i, 0)),
        ),
        out_shape=jax.ShapeDtypeStruct((vocab, cols), jnp.float32),
        compiler_params=params(),
        name="word_sums",
    )(starts, theta, weights, docs, rows, beta_high, beta_low)


def per_device(log_beta, gamma_init, topic_prior, word_block, word_row, counts):
    doc_rows, length = counts.shape
    vocab, cols = log_beta.shape
    owners = lax.axis_size("docs")
    tokens = doc_rows * length
    slots = 2 * tokens
    all_docs = owners * doc_rows
    block = min(512, vocab)
    chunk = min(256, slots)
    tile = min(1024, slots)

    sent = jnp.stack([word_block[:, :, 0] * vocab + word_row, counts])
    named = spread(sent, "docs")
    row = named[:, 0] - lax.axis_index("docs") * vocab
    count = named[:, 1]
    doc = (
        lax.broadcasted_iota(jnp.int32, row.shape, 0) * doc_rows
        + lax.broadcasted_iota(jnp.int32, row.shape, 1)
    )
    code = (row * all_docs + doc) * COUNT_SPAN + count
    none = jnp.int32(vocab * all_docs * COUNT_SPAN)
    mine = (row >= 0) & (row < vocab) & (count > 0)
    code = jnp.sort(jnp.where(mine, code, none).reshape(-1))[:slots]
    filled = code < none
    slot_count = jnp.where(filled, code % COUNT_SPAN, 0).astype(jnp.float32)
    slot_doc = jnp.where(filled, code // COUNT_SPAN % all_docs, all_docs)
    slot_row = code // (COUNT_SPAN * all_docs)
    bounds = jnp.arange(vocab // block + 1, dtype=jnp.int32) * (block * all_docs * COUNT_SPAN)
    starts = jnp.sum((code[None, :] < bounds[:, None]).astype(jnp.int32), axis=1)
    used = starts[-1:]
    lines = (slots // tile, 1, tile)
    rows2 = slot_row.reshape(slots // chunk, chunk)
    docs3 = slot_doc.reshape(lines)
    count3 = slot_count.reshape(lines)

    found = gather_rows(log_beta, rows2, starts, block, chunk)
    beta_high, beta_low, top = shifted_exp(found, used, tile)

    gamma = gamma_init
    for sweep in range(ITERS + 1):
        theta = jnp.exp(lax.digamma(gamma))
        theta_all = spread(theta, "docs").reshape(all_docs, cols)
        mass = slot_mass(theta_all, beta_high, beta_low, docs3, used, tile)
        if sweep == 0:
            pairs = spread(jnp.stack([top, mass]), "topics")
            tops = jnp.max(pairs[:, 0], axis=0)
            factor = jnp.exp(top - tops)
            total = jnp.sum(pairs[:, 1] * jnp.exp(pairs[:, 0] - tops[None]), axis=0)
        else:
            total = jnp.sum(spread(mass * factor, "topics"), axis=0)
        weights = jnp.where(count3 > 0, count3 * factor / total, 0.0)
        if sweep < ITERS:
            sums = doc_sums(weights, docs3, beta_high, beta_low, all_docs, used, tile)
            sums = lax.all_to_all(
                sums.reshape(owners, doc_rows, cols), "docs", split_axis=0, concat_axis=0, tiled=True
            )
            gamma = topic_prior[None, :] + theta * jnp.sum(sums, axis=0)
    sstats = word_sums(
        theta_all,
        weights.reshape(slots // chunk, chunk),
        slot_doc.reshape(slots // chunk, chunk),
        rows2,
        beta_high,
        beta_low,
        starts,
        vocab,
        block,
        chunk,
    )
    return (gamma, sstats)


def solution(mesh):
    in_specs = (
        P("docs", "topics"),
        P("docs", "topics"),
        P("topics"),
        P("docs", None, None),
        P("docs", None),
        P("docs", None),
    )
    out_specs = (P("docs", "topics"), P("docs", "topics"))
    return jax.shard_map(
        per_device, mesh=mesh, in_specs=in_specs, out_specs=out_specs, check_vma=False
    )
```
